32 devices in a mesh: row: 4 (over y, x), col: 8 (over z, core).
Axes of the slice: x: 2, y: 2, z: 4, core: 2. Of those that a mesh axis runs over, the one named last changes fastest.
Arguments:
- throat_owner: int32 [16384, 1], P(('row', 'col')), may hold values from 0 to 3; in each aligned block of 512 rows (0 to 511, 512 to 1023, ...) at most 128 rows name the same one
- throat_interior: int32 [16384], P(('row', 'col')), may hold values from 0 to 895
- throat_offset: int32 [16384], P(('row', 'col')), may hold values from 0 to 4095
- throat_conductance: float32 [16384], P(('row', 'col')), may hold values from 0.1 to 1
- child_update: bfloat16 [7168, 16384], P('col', 'row'), may hold values from -0.09375 to 0.09375
- panel_pores: int32 [4096], replicated, may hold values from 0 to 16383, as said below
- interior_inverse: bfloat16 [7168, 896], P('col'), as said below
- separator_rows: float32 [4096, 16384], P('col', 'row'), may hold values from -6 to 6
Outputs:
- schur_rows: float32 [4096, 16384], P('col', 'row')
The draws below stay inside these ranges and needn't reach their ends.
Inputs may be any that keep to these rules, and one draw needn't show every extreme that they name: `throat_owner`: in each device's block of 512 throats no owner is named more than 128 times, a bound that some block reaches. `panel_pores`: the 4096 pores are distinct; at most 1536 of them lie in any one owner's range of 4096 pores, and one owner holds exactly 1536. `interior_inverse`: each group's block of 896 rows is lower triangular with diagonal entries between 0.8 and 1.2.
All inputs are finite; a program needn't handle non-finite values.
Results may differ from the reference program's by a relative error of at most 0.01.
Values may be sent and summed in bfloat16 or wider, within the bound.
No kernel may reach another device: no remote copies, remote signals or barrier semaphores. Data moves between devices by JAX's collectives and lax.ppermute only.
A program may use at most 128 MiB of HBM per device.

```python
import math
import jax
import jax.numpy as jnp
import numpy as np
from jax import lax

SEP = 16384
PANEL = 4096
NIC = 896
TH_DEV = 512
CAPT = 128
CAP = 1536
NI = 7168
THROATS = 16384
N_ROW = 4
N_COL = 8


def draw_panel_pores(key, part):
    owner_width = SEP // N_ROW
    first_key, second_key, third_key = jax.random.split(jax.random.fold_in(key, 11), 3)
    owner_order = jax.random.permutation(first_key, N_ROW)
    others = (PANEL - CAP) // (N_ROW - 1)
    leftover = PANEL - CAP - others * (N_ROW - 1)
    placing = jnp.arange(N_ROW, dtype=jnp.int32)
    by_place = jnp.where(placing == 0, CAP, others + (placing - 1 < leftover).astype(jnp.int32)).astype(jnp.int32)
    counts = jnp.zeros((N_ROW,), jnp.int32).at[owner_order].set(by_place)
    ending = jnp.cumsum(counts)
    starts = ending - counts
    columns = jnp.arange(PANEL, dtype=jnp.int32)
    owner_of = jnp.sum((columns[:, None] >= ending[None, :]).astype(jnp.int32), axis=1)
    within = columns - starts[owner_of]
    shuffles = jax.vmap(lambda subkey: jax.random.permutation(subkey, owner_width))(jax.random.split(second_key, N_ROW))
    chosen = owner_of * owner_width + shuffles[owner_of, within]
    return chosen[jax.random.permutation(third_key, PANEL)].astype(jnp.int32)


def draw_interior_inverse(key, part):
    first_key, second_key = jax.random.split(jax.random.fold_in(key, 23))
    shape = (NIC * N_COL, NIC)
    local_row = (jnp.arange(NIC * N_COL) % NIC)[:, None]
    column = jnp.arange(NIC)[None, :]
    below = jax.random.normal(first_key, shape, jnp.float32) / jnp.sqrt(jnp.float32(NIC))
    diagonal = jax.random.uniform(second_key, shape, jnp.float32, 0.8, 1.2)
    return jnp.where(column < local_row, below, jnp.where(column == local_row, diagonal, 0.0)).astype(jnp.bfloat16)


def touch_ends(drawn, stream_key, low, largest):
    index_at = [jax.random.randint(jax.random.fold_in(stream_key, axis), (), 0, length) for axis, length in enumerate(drawn.shape)]
    longest = drawn.shape.index(max(drawn.shape))
    beside = index_at[:longest] + [(index_at[longest] + 1) % drawn.shape[longest]] + index_at[longest + 1:]
    return drawn.at[tuple(index_at)].set(low).at[tuple(beside)].set(largest)


def levels(key, shape, pieces, low, largest):
    gain, own = 1.0, jax.random.fold_in(key, 6)
    for axis_at, shards_of in pieces:
        draws = jnp.exp(jax.random.uniform(jax.random.fold_in(own, axis_at), (shards_of,), jnp.float32, low / len(pieces), largest / len(pieces)))
        gain = gain * jnp.repeat(draws, shape[axis_at] // shards_of).reshape([-1 if axis == axis_at else 1 for axis in range(len(shape))])
    return gain


def assign_block(stream_key, own, number, rows, number_of, top, reach, lean):
    sequence = jax.random.permutation(stream_key, number_of)
    heavy_load, usual = shares(number_of, rows * top, reach, lean, True), shares(number_of, rows * top, reach, lean, False)
    places = jnp.arange(number_of)

    def named(lengths, rotation):
        used = int((lengths > 0).sum())
        fixed = max(1, used // 4)
        moved = fixed + (places - fixed + rotation * (used - fixed)) % max(1, number_of - fixed)
        return jnp.zeros((number_of,), jnp.int32).at[sequence[jnp.where(places < fixed, places, moved)]].set(jnp.asarray(lengths, jnp.int32))

    lengths = jnp.where(number % 4 == 0, named(heavy_load, number // 4), named(usual, number - number // 4 - 1))
    mixed = jax.random.permutation(jax.random.fold_in(own, 3), number_of)
    donor, sink = mixed[0:number_of // 2 * 2:2], mixed[1:number_of // 2 * 2:2]
    room = jnp.minimum(lengths[donor] - 1, reach - lengths[sink]) // 2
    room = jnp.where((donor == sequence[0]) | (sink == sequence[0]) | (lengths[sink] == 0), 0, jnp.maximum(room, 0))
    moved = jax.random.randint(jax.random.fold_in(own, 4), (number_of // 2,), 0, 1 << 20) % (room + 1)
    lengths = lengths.at[donor].add(-moved).at[sink].add(moved)
    labels = jnp.searchsorted(jnp.cumsum(lengths), jnp.arange(rows * top), side="right").astype(jnp.int32)
    listing = labels.reshape(top, rows).T
    listing = listing[jax.random.permutation(jax.random.fold_in(own, 1), rows)]
    rotation = jax.random.randint(jax.random.fold_in(own, 2), (rows, 1), 0, top)
    return jnp.take_along_axis(listing, (jnp.arange(top)[None, :] + rotation) % top, axis=1)


def shares(amount, total, bound, skew, full):
    portions = [(1 << 20) // math.isqrt(standing ** skew) + 1 for standing in range(1, amount + 1)]
    largest = bound if full else min(bound, max(-(-total // amount), total * portions[0] // sum(portions)))
    least = 1 if total - largest >= amount - 1 else 0
    given, surplus = [largest] + [least] * (amount - 1), total - largest - least * (amount - 1)
    while surplus > 0:
        candidates = [i for i in range(1, amount) if given[i] < largest] or [i for i in range(1, amount) if given[i] < bound]
        pool, remaining = sum([portions[i] for i in candidates]), surplus
        for i in candidates:
            addition = min(bound - given[i], max(1, remaining * portions[i] // pool), surplus)
            given[i] = given[i] + addition
            surplus = surplus - addition
    return np.array(given)


def gaussian(stream_key, shape, deviation, most, cuts=(), kind=jnp.bfloat16):
    gain = levels(stream_key, shape, cuts, -0.22, 0.18) if cuts else 1.0
    entries = jax.random.normal(stream_key, shape, jnp.float32) * deviation * gain
    return jnp.minimum(jnp.maximum(entries, -most), most).astype(kind)


def setup_inputs(seed: int = 0) -> dict:
    splits = jax.random.split(jax.random.key(seed), 9)
    throat_owner_keys = jax.random.split(jax.random.fold_in(splits[0], 1), THROATS // TH_DEV)
    throat_owner_turns = jax.random.permutation(jax.random.fold_in(splits[0], 3), THROATS // TH_DEV)
    throat_owner = jax.vmap(lambda own, number: assign_block(jax.random.fold_in(splits[0], 2), own, number, TH_DEV, N_ROW, 1, CAPT, 2))(throat_owner_keys, throat_owner_turns).reshape((THROATS, 1))
    throat_interior = touch_ends(jax.random.randint(splits[1], (THROATS,), 0, NIC), jax.random.fold_in(splits[1], 1), 0, NIC - 1).astype(jnp.int32)
    throat_offset = touch_ends(jax.random.randint(splits[2], (THROATS,), 0, SEP // N_ROW), jax.random.fold_in(splits[2], 1), 0, (SEP // N_ROW) - 1).astype(jnp.int32)
    throat_conductance = jnp.clip(jnp.exp(math.log(1.0) - 2.3025851 * jax.random.uniform(splits[3], (THROATS,), jnp.float32) ** levels(splits[3], (THROATS,), ((0, 32),), -0.2, 0.2)), 0.1, 1.0)
    child_update = gaussian(splits[4], (NI, SEP), (4 * NIC) ** -0.5, 0.09375, ((0, 8), (1, 4)))
    panel_pores = draw_panel_pores(jax.random.fold_in(splits[8], 71), 0)
    interior_inverse = draw_interior_inverse(jax.random.fold_in(splits[8], 71), 0)
    separator_rows = gaussian(splits[7], (PANEL, SEP), 1.0, 6.0, ((0, 8), (1, 4)), jnp.float32)
    return {"throat_owner": throat_owner, "throat_interior": throat_interior, "throat_offset": throat_offset, "throat_conductance": throat_conductance, "child_update": child_update, "panel_pores": panel_pores, "interior_inverse": interior_inverse, "separator_rows": separator_rows}


def reference(throat_owner, throat_interior, throat_offset, throat_conductance, child_update, panel_pores, interior_inverse, separator_rows):
    owner_width = SEP // N_ROW
    throat_pores = throat_owner[:, 0] * owner_width + throat_offset

    def grouped(values):
        return values.reshape(N_ROW, N_COL, TH_DEV).transpose(1, 0, 2).reshape(N_COL, N_ROW * TH_DEV)

    inverses = interior_inverse.reshape(N_COL, NIC, NIC)
    fills = child_update.reshape(N_COL, NIC, SEP)

    def accumulate(running, inputs):
        group_pores, group_rows, group_values, inverse, fill = inputs
        summed = fill.astype(jnp.float32).at[group_rows, group_pores].add(group_values)
        coupling = summed.astype(jnp.bfloat16)
        solved = jnp.dot(inverse, coupling, preferred_element_type=jnp.float32).astype(jnp.bfloat16)
        panel_block = jnp.take(solved, panel_pores, axis=1)
        product = jnp.dot(panel_block.T, solved, preferred_element_type=jnp.float32).astype(jnp.bfloat16)
        product = lax.optimization_barrier(product)
        return running + product.astype(jnp.float32), None

    running, unused = lax.scan(accumulate, jnp.zeros((PANEL, SEP), jnp.float32), (grouped(throat_pores), grouped(throat_interior), grouped(throat_conductance), inverses, fills))
    return separator_rows - running
```

```python
import jax
import jax.numpy as jnp
from jax import lax
from jax.sharding import PartitionSpec as P

STEPS = (2, 3, 3, 4, 5, 6, 5, 3, 1)


def route_throats(owners, interior, offset, conductance, row_count, owner_width):
    throats = interior.shape[0]
    slot_limit = throats // 4
    order = jnp.arange(throats, dtype=jnp.int32)
    earlier = (owners[None, :] == owners[:, None]) & (order[None, :] < order[:, None])
    rank = jnp.sum(earlier.astype(jnp.int32), axis=1)
    slot = owners * slot_limit + rank
    code = (interior * owner_width + offset + 1).astype(jnp.float32)
    slots = jnp.arange(row_count * slot_limit, dtype=jnp.int32)
    placed = slots[:, None] == slot[None, :]
    codes = jnp.sum(jnp.where(placed, code[None, :], 0.0), axis=1)
    values = jnp.sum(jnp.where(placed, conductance[None, :], 0.0), axis=1)
    block = jnp.stack(
        [codes.reshape(row_count, slot_limit), values.reshape(row_count, slot_limit)], axis=1
    )
    back = lax.all_to_all(block, "row", split_axis=0, concat_axis=0, tiled=True)
    codes = back[:, 0, :].reshape(-1).astype(jnp.int32) - 1
    values = back[:, 1, :].reshape(-1)
    return codes // owner_width, codes % owner_width, values


def add_throats(child_update, pivots, pores, values):
    high = lax.reduce_precision(values, 8, 7)
    low = values - high
    values = jnp.concatenate([high, low]).astype(jnp.bfloat16)
    pivots = jnp.concatenate([pivots, pivots])
    pores = jnp.concatenate([pores, pores])
    rows = jnp.arange(child_update.shape[0], dtype=jnp.int32)
    columns = jnp.arange(child_update.shape[1], dtype=jnp.int32)
    left = jnp.where(rows[:, None] == pivots[None, :], values[None, :], jnp.bfloat16(0))
    right = (pores[:, None] == columns[None, :]).astype(jnp.bfloat16)
    summed = jnp.dot(left, right, preferred_element_type=jnp.float32)
    return (child_update.astype(jnp.float32) + summed).astype(jnp.bfloat16)


def per_device(
    throat_owner,
    throat_interior,
    throat_offset,
    throat_conductance,
    child_update,
    panel_pores,
    interior_inverse,
    separator_rows,
):
    row_count = lax.axis_size("row")
    col_count = lax.axis_size("col")
    row_index = lax.axis_index("row")
    col_index = lax.axis_index("col")
    own_rows, owner_width = separator_rows.shape
    chips = col_count // 2
    core = col_index % 2
    chip = col_index // 2
    square = row_count == 4
    line = chips == 4
    at_end = (chip == 0) | (chip == chips - 1)

    pivots, pores, values = route_throats(
        throat_owner[:, 0],
        throat_interior,
        throat_offset,
        throat_conductance,
        row_count,
        owner_width,
    )
    coupling = add_throats(child_update, pivots, pores, values)
    solved = jnp.dot(interior_inverse, coupling, preferred_element_type=jnp.float32).astype(
        jnp.bfloat16
    )

    local_pores = (panel_pores - row_index * owner_width).reshape(chips, 2, own_rows)
    if line:
        order = jnp.array([[0, 1, 2, 3], [1, 2, 3, 0], [2, 1, 0, 3], [3, 2, 1, 0]], jnp.int32)
        local_pores = jnp.take(local_pores, order[chip], axis=0)
    other_pores = jnp.where(core == 0, local_pores[:, 1], local_pores[:, 0])
    mine_pores = jnp.where(core == 0, local_pores[:, 0], local_pores[:, 1])
    columns = jnp.arange(owner_width, dtype=jnp.int32)

    swap = [(i, i ^ 1) for i in range(col_count)]
    along_x = [(i, i ^ 1) for i in range(row_count)]
    along_y = [(i, i ^ 2) for i in range(row_count)]
    ends = [(i, i ^ 2) for i in range(col_count)]
    outward = [(2 * g + c, 2 * t + c) for g, t in ((1, 0), (2, 3)) for c in range(2)]
    across = [(2 * g + c, 2 * t + c) for g, t in ((0, 0), (1, 2), (2, 1), (3, 3)) for c in range(2)]

    sizes = [own_rows * s // sum(STEPS) for s in STEPS]
    starts = [sum(sizes[:i]) for i in range(len(sizes))]
    count = len(sizes)
    state = [dict() for _ in sizes]

    def pick(s, k):
        part = slice(starts[k], starts[k] + sizes[k])
        parts = [other_pores[:, part].reshape(-1), mine_pores[:, part].reshape(-1)]
        onehot = (jnp.concatenate(parts)[:, None] == columns[None, :]).astype(jnp.bfloat16)
        rows = lax.dot_general(
            onehot, shared["solved"], (((1,), (1,)), ((), ())), preferred_element_type=jnp.float32
        ).astype(jnp.bfloat16)
        half = chips * sizes[k]
        s["first"], s["second"] = rows[:half], rows[half:]

    def share(s, k):
        if square:
            s["first_in"] = lax.ppermute(s["first"], "row", along_x)
            s["second_in"] = lax.ppermute(s["second"], "row", along_y)
        else:
            s["first"] = lax.psum(s["first"], "row")
            s["second"] = lax.psum(s["second"], "row")

    def share_again(s, k):
        if square:
            s["first"] += s.pop("first_in")
            s["second"] += s.pop("second_in")
            s["first_in"] = lax.ppermute(s["first"], "row", along_y)
            s["second_in"] = lax.ppermute(s["second"], "row", along_x)

    def multiply(s, k):
        first, second = s.pop("first"), s.pop("second")
        if square:
            first += s.pop("first_in")
            second += s.pop("second_in")
        sent, mine = (
            jnp.dot(rows, shared["solved"], preferred_element_type=jnp.float32).astype(jnp.bfloat16)
            for rows in (first, second)
        )
        n = sizes[k]
        come = lax.ppermute(sent, "col", swap)
        s["own"] = mine[:n] + come[:n]
        s["rest"] = mine[n:] + come[n:]

    def rides(k):
        return k + LATER < count and sizes[k] <= 3 * sizes[k + LATER]

    def leaving(k):
        s, n = state[k], sizes[k]
        return s.pop("rest")[2 * n :] + s["from_middle"][n:]

    def move_in(s, k):
        if line:
            sent = s["rest"]
            if k >= LATER and rides(k - LATER):
                out = leaving(k - LATER)
                n = out.shape[0]
                sent = jnp.concatenate([jnp.where(at_end, sent[:n], out), sent[n:]], axis=0)
            flying[k] = lax.ppermute(sent, "col", ends)

    def land(s, k):
        if line:
            s["from_end"] = flying.pop(k)

    def move_across(s, k):
        if line:
            n = sizes[k]
            s["from_middle"] = lax.ppermute(s["rest"][: 2 * n] + s["from_end"][n:], "col", across)

    def move_out(s, k):
        if line and not rides(k):
            s["from_inner"] = lax.ppermute(leaving(k), "col", outward)

    def settle(s, k):
        n = sizes[k]
        own = s.pop("own")
        if line:
            here = s["from_end"][:n].astype(jnp.float32) + s["from_middle"][:n].astype(jnp.float32)
            there = state[k + LATER]["from_end"][:n] if rides(k) else s["from_inner"]
            update = own.astype(jnp.float32) + jnp.where(at_end, there.astype(jnp.float32), here)
        else:
            groups = [[2 * g + c for g in range(chips)] for c in range(2)]
            pair = jnp.concatenate([own, s["rest"]], axis=0)
            update = lax.psum_scatter(
                pair, "col", scatter_dimension=0, axis_index_groups=groups, tiled=True
            ).astype(jnp.float32)
        rows = lax.slice_in_dim(shared["out"], starts[k], starts[k] + n, axis=0)
        shared["out"] = lax.dynamic_update_slice(shared["out"], rows - update, (starts[k], 0))

    stages = {
        0: (pick,),
        1: (share,),
        2: (share_again,),
        3: (multiply,),
        4: (move_in,),
        6: (land, move_across),
        7: (move_out,),
    }
    LATER = 3
    shared = {"solved": solved, "out": separator_rows}
    flying = {}
    for turn in range(count + 9):
        shared, state = lax.optimization_barrier((shared, state))
        for k in reversed(range(count)):
            for stage in stages.get(turn - k, ()):
                stage(state[k], k)
            if turn - k == (9 if rides(k) else 8):
                settle(state[k], k)
    return shared["out"]


def solution(mesh):
    in_specs = (
        P(("row", "col"), None),
        P(("row", "col")),
        P(("row", "col")),
        P(("row", "col")),
        P("col", "row"),
        P(),
        P("col", None),
        P("col", "row"),
    )
    out_specs = P("col", "row")
    return jax.shard_map(
        per_device, mesh=mesh, in_specs=in_specs, out_specs=out_specs, check_vma=False
    )
```

```python
import jax
import jax.numpy as jnp
from jax import lax
from jax.sharding import PartitionSpec as P

STEPS = (3, 3, 4, 4, 4, 4, 4, 3, 2, 1)
LATER = 3
STAYS = 0
ALONE = 3


def route_throats(owners, interior, offset, conductance, row_count, owner_width):
    throats = interior.shape[0]
    slot_limit = throats // 4
    order = jnp.arange(throats, dtype=jnp.int32)
    earlier = (owners[None, :] == owners[:, None]) & (order[None, :] < order[:, None])
    rank = jnp.sum(earlier.astype(jnp.int32), axis=1)
    slot = owners * slot_limit + rank
    code = (interior * owner_width + offset + 1).astype(jnp.float32)
    slots = jnp.arange(row_count * slot_limit, dtype=jnp.int32)
    placed = slots[:, None] == slot[None, :]
    codes = jnp.sum(jnp.where(placed, code[None, :], 0.0), axis=1)
    values = jnp.sum(jnp.where(placed, conductance[None, :], 0.0), axis=1)
    block = jnp.stack(
        [codes.reshape(row_count, slot_limit), values.reshape(row_count, slot_limit)], axis=1
    )
    back = lax.all_to_all(block, "row", split_axis=0, concat_axis=0, tiled=True)
    codes = back[:, 0, :].reshape(-1).astype(jnp.int32) - 1
    values = back[:, 1, :].reshape(-1)
    return codes // owner_width, codes % owner_width, values


def add_throats(child_update, pivots, pores, values):
    high = lax.reduce_precision(values, 8, 7)
    low = values - high
    values = jnp.concatenate([high, low]).astype(jnp.bfloat16)
    pivots = jnp.concatenate([pivots, pivots])
    pores = jnp.concatenate([pores, pores])
    rows = jnp.arange(child_update.shape[0], dtype=jnp.int32)
    columns = jnp.arange(child_update.shape[1], dtype=jnp.int32)
    left = jnp.where(rows[:, None] == pivots[None, :], values[None, :], jnp.bfloat16(0))
    right = (pores[:, None] == columns[None, :]).astype(jnp.bfloat16)
    summed = jnp.dot(left, right, preferred_element_type=jnp.float32)
    return (child_update.astype(jnp.float32) + summed).astype(jnp.bfloat16)


def per_device(
    throat_owner,
    throat_interior,
    throat_offset,
    throat_conductance,
    child_update,
    panel_pores,
    interior_inverse,
    separator_rows,
):
    row_count = lax.axis_size("row")
    col_count = lax.axis_size("col")
    row_index = lax.axis_index("row")
    col_index = lax.axis_index("col")
    own_rows, owner_width = separator_rows.shape
    chips = col_count // 2
    core = col_index % 2
    chip = col_index // 2
    square = row_count == 4
    line = chips == 4
    at_end = (chip == 0) | (chip == chips - 1)

    pivots, pores, values = route_throats(
        throat_owner[:, 0],
        throat_interior,
        throat_offset,
        throat_conductance,
        row_count,
        owner_width,
    )
    coupling = add_throats(child_update, pivots, pores, values)
    solved = jnp.dot(interior_inverse, coupling, preferred_element_type=jnp.float32).astype(
        jnp.bfloat16
    )

    local_pores = (panel_pores - row_index * owner_width).reshape(chips, 2, own_rows)
    if line:
        order = jnp.array([[0, 1, 2, 3], [1, 2, 3, 0], [2, 1, 0, 3], [3, 2, 1, 0]], jnp.int32)
        local_pores = jnp.take(local_pores, order[chip], axis=0)
    other_pores = jnp.where(core == 0, local_pores[:, 1], local_pores[:, 0])
    mine_pores = jnp.where(core == 0, local_pores[:, 0], local_pores[:, 1])
    columns = jnp.arange(owner_width, dtype=jnp.int32)

    swap = [(i, i ^ 1) for i in range(col_count)]
    along_x = [(i, i ^ 1) for i in range(row_count)]
    along_y = [(i, i ^ 2) for i in range(row_count)]
    ends = [(i, i ^ 2) for i in range(col_count)]
    inward = [(2 * g + c, 2 * t + c) for g, t in ((0, 1), (3, 2)) for c in range(2)]
    outward = [(2 * g + c, 2 * t + c) for g, t in ((1, 0), (2, 3)) for c in range(2)]
    across = [(2 * g + c, 2 * t + c) for g, t in ((0, 0), (1, 2), (2, 1), (3, 3)) for c in range(2)]

    sizes = [own_rows * s // sum(STEPS) for s in STEPS]
    starts = [sum(sizes[:i]) for i in range(len(sizes))]
    count = len(sizes)
    state = [dict() for _ in sizes]

    def pick(k):
        part = slice(starts[k], starts[k] + sizes[k])
        pores = jnp.concatenate([other_pores[:, part].reshape(-1), mine_pores[:, part].reshape(-1)])
        onehot = (pores[:, None] == columns[None, :]).astype(jnp.bfloat16)
        state[k]["rows"] = lax.dot_general(
            onehot, shared["solved"], (((1,), (1,)), ((), ())), preferred_element_type=jnp.float32
        ).astype(jnp.bfloat16)

    def share(k):
        s = state[k]
        if square:
            s["rows_in"] = lax.ppermute(s["rows"], "row", along_x)
        else:
            s["rows"] = lax.psum(s["rows"], "row")

    def share_again(k):
        s = state[k]
        if square:
            s["rows"] += s.pop("rows_in")
            s["rows_in"] = lax.ppermute(s["rows"], "row", along_y)

    def multiply(k):
        s = state[k]
        rows = s.pop("rows")
        if square:
            rows += s.pop("rows_in")
        half = chips * sizes[k]
        sent, mine = (
            jnp.dot(picked, shared["solved"], preferred_element_type=jnp.float32).astype(jnp.bfloat16)
            for picked in (rows[:half], rows[half:])
        )
        n = sizes[k]
        come = lax.ppermute(sent, "col", swap)
        s["own"] = mine[:n] + come[:n]
        s["rest"] = mine[n:] + come[n:]

    def rides(k):
        return k + LATER < count - ALONE

    def leaving(k):
        s, n = state[k], sizes[k]
        return s.pop("rest")[2 * n :] + s["from_middle"][n:]

    def move_in(k):
        s = state[k]
        if line:
            sent = s["rest"]
            if k >= LATER and rides(k - LATER):
                out = leaving(k - LATER)
                n = out.shape[0]
                sent = jnp.concatenate([jnp.where(at_end, sent[:n], out), sent[n:]], axis=0)
            come = lax.ppermute(sent, "col", ends if k < count - ALONE else inward)
            if k < STAYS:
                s["from_end"] = come
            else:
                flying[k] = come

    def land(k):
        s = state[k]
        if k in flying:
            s["from_end"] = flying.pop(k)

    def move_across(k):
        s = state[k]
        if line:
            n = sizes[k]
            s["from_middle"] = lax.ppermute(s["rest"][: 2 * n] + s["from_end"][n:], "col", across)

    def move_out(k):
        s = state[k]
        if line and not rides(k):
            s["from_inner"] = lax.ppermute(leaving(k), "col", outward)

    def settle(k):
        s = state[k]
        n = sizes[k]
        own = s.pop("own")
        if line:
            here = s["from_end"][:n].astype(jnp.float32) + s["from_middle"][:n].astype(jnp.float32)
            there = state[k + LATER]["from_end"][:n] if rides(k) else s["from_inner"]
            update = own.astype(jnp.float32) + jnp.where(at_end, there.astype(jnp.float32), here)
        else:
            groups = [[2 * g + c for g in range(chips)] for c in range(2)]
            pair = jnp.concatenate([own, s["rest"]], axis=0)
            update = lax.psum_scatter(
                pair, "col", scatter_dimension=0, axis_index_groups=groups, tiled=True
            ).astype(jnp.float32)
        rows = lax.slice_in_dim(shared["out"], starts[k], starts[k] + n, axis=0)
        shared["out"] = lax.dynamic_update_slice(shared["out"], rows - update, (starts[k], 0))

    plan = {}

    def at(turn, stage, *args):
        plan.setdefault(turn, []).append((stage, args))

    for k in reversed(range(count)):
        at(k, pick, k)
        at(k + 1, share, k)
        at(k + 2, share_again, k)
        at(k + 6, land, k)
    for k in reversed(range(count)):
        at(k + 3, multiply, k)
        at(k + 6, move_across, k)
        at(k + 4, move_in, k)
        if not rides(k):
            at(k + 7, move_out, k)
        at(k + (9 if rides(k) else 8), settle, k)
    shared = {"solved": solved, "out": separator_rows}
    flying = {}
    for turn in range(max(plan) + 1):
        shared, state = lax.optimization_barrier((shared, state))
        for stage, args in plan.get(turn, ()):
            stage(*args)
    return shared["out"]


def solution(mesh):
    in_specs = (
        P(("row", "col"), None),
        P(("row", "col")),
        P(("row", "col")),
        P(("row", "col")),
        P("col", "row"),
        P(),
        P("col", None),
        P("col", "row"),
    )
    out_specs = P("col", "row")
    return jax.shard_map(
        per_device, mesh=mesh, in_specs=in_specs, out_specs=out_specs, check_vma=False
    )
```

```python
import jax
import jax.numpy as jnp
from jax import lax
from jax.sharding import PartitionSpec as P

STEPS = (3, 3, 4, 4, 4, 4, 4, 3, 2, 1)
LATER = 3
STAYS = 1
ALONE = 2


def route_throats(owners, interior, offset, conductance, row_count, owner_width):
    throats = interior.shape[0]
    slot_limit = throats // 4
    order = jnp.arange(throats, dtype=jnp.int32)
    earlier = (owners[None, :] == owners[:, None]) & (order[None, :] < order[:, None])
    rank = jnp.sum(earlier.astype(jnp.int32), axis=1)
    slot = owners * slot_limit + rank
    code = (interior * owner_width + offset + 1).astype(jnp.float32)
    slots = jnp.arange(row_count * slot_limit, dtype=jnp.int32)
    placed = slots[:, None] == slot[None, :]
    codes = jnp.sum(jnp.where(placed, code[None, :], 0.0), axis=1)
    values = jnp.sum(jnp.where(placed, conductance[None, :], 0.0), axis=1)
    block = jnp.stack(
        [codes.reshape(row_count, slot_limit), values.reshape(row_count, slot_limit)], axis=1
    )
    back = lax.all_to_all(block, "row", split_axis=0, concat_axis=0, tiled=True)
    codes = back[:, 0, :].reshape(-1).astype(jnp.int32) - 1
    values = back[:, 1, :].reshape(-1)
    return codes // owner_width, codes % owner_width, values


def add_throats(child_update, pivots, pores, values):
    high = lax.reduce_precision(values, 8, 7)
    low = values - high
    values = jnp.concatenate([high, low]).astype(jnp.bfloat16)
    pivots = jnp.concatenate([pivots, pivots])
    pores = jnp.concatenate([pores, pores])
    rows = jnp.arange(child_update.shape[0], dtype=jnp.int32)
    columns = jnp.arange(child_update.shape[1], dtype=jnp.int32)
    left = jnp.where(rows[:, None] == pivots[None, :], values[None, :], jnp.bfloat16(0))
    right = (pores[:, None] == columns[None, :]).astype(jnp.bfloat16)
    summed = jnp.dot(left, right, preferred_element_type=jnp.float32)
    return (child_update.astype(jnp.float32) + summed).astype(jnp.bfloat16)


def per_device(
    throat_owner,
    throat_interior,
    throat_offset,
    throat_conductance,
    child_update,
    panel_pores,
    interior_inverse,
    separator_rows,
):
    row_count = lax.axis_size("row")
    col_count = lax.axis_size("col")
    row_index = lax.axis_index("row")
    col_index = lax.axis_index("col")
    own_rows, owner_width = separator_rows.shape
    chips = col_count // 2
    core = col_index % 2
    chip = col_index // 2
    square = row_count == 4
    line = chips == 4
    at_end = (chip == 0) | (chip == chips - 1)

    pivots, pores, values = route_throats(
        throat_owner[:, 0],
        throat_interior,
        throat_offset,
        throat_conductance,
        row_count,
        owner_width,
    )
    coupling = add_throats(child_update, pivots, pores, values)
    solved = jnp.dot(interior_inverse, coupling, preferred_element_type=jnp.float32).astype(
        jnp.bfloat16
    )

    local_pores = (panel_pores - row_index * owner_width).reshape(chips, 2, own_rows)
    if line:
        order = jnp.array([[0, 1, 2, 3], [1, 2, 3, 0], [2, 1, 0, 3], [3, 2, 1, 0]], jnp.int32)
        local_pores = jnp.take(local_pores, order[chip], axis=0)
    other_pores = jnp.where(core == 0, local_pores[:, 1], local_pores[:, 0])
    mine_pores = jnp.where(core == 0, local_pores[:, 0], local_pores[:, 1])
    columns = jnp.arange(owner_width, dtype=jnp.int32)

    swap = [(i, i ^ 1) for i in range(col_count)]
    along_x = [(i, i ^ 1) for i in range(row_count)]
    along_y = [(i, i ^ 2) for i in range(row_count)]
    ends = [(i, i ^ 2) for i in range(col_count)]
    inward = [(2 * g + c, 2 * t + c) for g, t in ((0, 1), (3, 2)) for c in range(2)]
    outward = [(2 * g + c, 2 * t + c) for g, t in ((1, 0), (2, 3)) for c in range(2)]
    across = [(2 * g + c, 2 * t + c) for g, t in ((1, 2), (2, 1)) for c in range(2)]

    sizes = [own_rows * s // sum(STEPS) for s in STEPS]
    starts = [sum(sizes[:i]) for i in range(len(sizes))]
    count = len(sizes)
    state = [dict() for _ in sizes]

    def pick(k):
        part = slice(starts[k], starts[k] + sizes[k])
        pores = jnp.concatenate([other_pores[:, part].reshape(-1), mine_pores[:, part].reshape(-1)])
        onehot = (pores[:, None] == columns[None, :]).astype(jnp.bfloat16)
        state[k]["rows"] = lax.dot_general(
            onehot, shared["solved"], (((1,), (1,)), ((), ())), preferred_element_type=jnp.float32
        ).astype(jnp.bfloat16)

    def share(k):
        s = state[k]
        if square:
            s["rows_in"] = lax.ppermute(s["rows"], "row", along_x)
        else:
            s["rows"] = lax.psum(s["rows"], "row")

    def share_again(k):
        s = state[k]
        if square:
            s["rows"] += s.pop("rows_in")
            s["rows_in"] = lax.ppermute(s["rows"], "row", along_y)

    def multiply(k):
        s = state[k]
        rows = s.pop("rows")
        if square:
            rows += s.pop("rows_in")
        half = chips * sizes[k]
        sent, mine = (
            jnp.dot(picked, shared["solved"], preferred_element_type=jnp.float32).astype(jnp.bfloat16)
            for picked in (rows[:half], rows[half:])
        )
        n = sizes[k]
        come = lax.ppermute(sent, "col", swap)
        s["own"] = mine[:n] + come[:n]
        s["rest"] = mine[n:] + come[n:]

    def rides(k):
        return k + LATER < count - ALONE

    def leaving(k):
        s, n = state[k], sizes[k]
        return s.pop("rest")[2 * n :] + s["from_middle"][n:]

    def move_in(k):
        s = state[k]
        if line:
            sent = s["rest"]
            if k >= LATER and rides(k - LATER):
                out = leaving(k - LATER)
                n = out.shape[0]
                sent = jnp.concatenate([jnp.where(at_end, sent[:n], out), sent[n:]], axis=0)
            come = lax.ppermute(sent, "col", ends if k < count - ALONE else inward)
            if k < STAYS:
                s["from_end"] = come
            else:
                flying[k] = come

    def land(k):
        s = state[k]
        if k in flying:
            s["from_end"] = flying.pop(k)

    def move_across(k):
        s = state[k]
        if line:
            n = sizes[k]
            s["from_middle"] = lax.ppermute(s["rest"][: 2 * n] + s["from_end"][n:], "col", across)

    def move_out(k):
        s = state[k]
        if line and not rides(k):
            s["from_inner"] = lax.ppermute(leaving(k), "col", outward)

    def settle(k):
        s = state[k]
        n = sizes[k]
        own = s.pop("own")
        if line:
            here = s["from_end"][:n].astype(jnp.float32) + s["from_middle"][:n].astype(jnp.float32)
            there = state[k + LATER]["from_end"][:n] if rides(k) else s["from_inner"]
            update = own.astype(jnp.float32) + jnp.where(at_end, there.astype(jnp.float32), here)
        else:
            groups = [[2 * g + c for g in range(chips)] for c in range(2)]
            pair = jnp.concatenate([own, s["rest"]], axis=0)
            update = lax.psum_scatter(
                pair, "col", scatter_dimension=0, axis_index_groups=groups, tiled=True
            ).astype(jnp.float32)
        rows = lax.slice_in_dim(shared["out"], starts[k], starts[k] + n, axis=0)
        shared["out"] = lax.dynamic_update_slice(shared["out"], rows - update, (starts[k], 0))

    plan = {}

    def at(turn, stage, *args):
        plan.setdefault(turn, []).append((stage, args))

    for k in reversed(range(count)):
        at(k, pick, k)
        at(k + 1, share, k)
        at(k + 2, share_again, k)
        at(k + 6, land, k)
    for k in reversed(range(count)):
        at(k + 3, multiply, k)
        at(k + 6, move_across, k)
        at(k + 4, move_in, k)
        if not rides(k):
            at(k + 7, move_out, k)
        at(k + (9 if rides(k) else 8), settle, k)
    shared = {"solved": solved, "out": separator_rows}
    flying = {}
    for turn in range(max(plan) + 1):
        shared, state = lax.optimization_barrier((shared, state))
        for stage, args in plan.get(turn, ()):
            stage(*args)
    return shared["out"]


def solution(mesh):
    in_specs = (
        P(("row", "col"), None),
        P(("row", "col")),
        P(("row", "col")),
        P(("row", "col")),
        P("col", "row"),
        P(),
        P("col", None),
        P("col", "row"),
    )
    out_specs = P("col", "row")
    return jax.shard_map(
        per_device, mesh=mesh, in_specs=in_specs, out_specs=out_specs, check_vma=False
    )
```

```python
import jax
import jax.numpy as jnp
from jax import lax
from jax.sharding import PartitionSpec as P

STEPS = (3, 3, 4, 4, 4, 4, 4, 3, 2, 1)
LATER = 3
STAYS = 1
ALONE = 1


def route_throats(owners, interior, offset, conductance, row_count, owner_width):
    throats = interior.shape[0]
    slot_limit = throats // 4
    order = jnp.arange(throats, dtype=jnp.int32)
    earlier = (owners[None, :] == owners[:, None]) & (order[None, :] < order[:, None])
    rank = jnp.sum(earlier.astype(jnp.int32), axis=1)
    slot = owners * slot_limit + rank
    code = (interior * owner_width + offset + 1).astype(jnp.float32)
    slots = jnp.arange(row_count * slot_limit, dtype=jnp.int32)
    placed = slots[:, None] == slot[None, :]
    codes = jnp.sum(jnp.where(placed, code[None, :], 0.0), axis=1)
    values = jnp.sum(jnp.where(placed, conductance[None, :], 0.0), axis=1)
    block = jnp.stack(
        [codes.reshape(row_count, slot_limit), values.reshape(row_count, slot_limit)], axis=1
    )
    back = lax.all_to_all(block, "row", split_axis=0, concat_axis=0, tiled=True)
    codes = back[:, 0, :].reshape(-1).astype(jnp.int32) - 1
    values = back[:, 1, :].reshape(-1)
    return codes // owner_width, codes % owner_width, values


def add_throats(child_update, pivots, pores, values):
    high = lax.reduce_precision(values, 8, 7)
    low = values - high
    values = jnp.concatenate([high, low]).astype(jnp.bfloat16)
    pivots = jnp.concatenate([pivots, pivots])
    pores = jnp.concatenate([pores, pores])
    rows = jnp.arange(child_update.shape[0], dtype=jnp.int32)
    columns = jnp.arange(child_update.shape[1], dtype=jnp.int32)
    left = jnp.where(rows[:, None] == pivots[None, :], values[None, :], jnp.bfloat16(0))
    right = (pores[:, None] == columns[None, :]).astype(jnp.bfloat16)
    summed = jnp.dot(left, right, preferred_element_type=jnp.float32)
    return (child_update.astype(jnp.float32) + summed).astype(jnp.bfloat16)


def per_device(
    throat_owner,
    throat_interior,
    throat_offset,
    throat_conductance,
    child_update,
    panel_pores,
    interior_inverse,
    separator_rows,
):
    row_count = lax.axis_size("row")
    col_count = lax.axis_size("col")
    row_index = lax.axis_index("row")
    col_index = lax.axis_index("col")
    own_rows, owner_width = separator_rows.shape
    chips = col_count // 2
    core = col_index % 2
    chip = col_index // 2
    square = row_count == 4
    line = chips == 4
    at_end = (chip == 0) | (chip == chips - 1)

    pivots, pores, values = route_throats(
        throat_owner[:, 0],
        throat_interior,
        throat_offset,
        throat_conductance,
        row_count,
        owner_width,
    )
    coupling = add_throats(child_update, pivots, pores, values)
    solved = jnp.dot(interior_inverse, coupling, preferred_element_type=jnp.float32).astype(
        jnp.bfloat16
    )

    local_pores = (panel_pores - row_index * owner_width).reshape(chips, 2, own_rows)
    if line:
        order = jnp.array([[0, 1, 2, 3], [1, 2, 3, 0], [2, 1, 0, 3], [3, 2, 1, 0]], jnp.int32)
        local_pores = jnp.take(local_pores, order[chip], axis=0)
    other_pores = jnp.where(core == 0, local_pores[:, 1], local_pores[:, 0])
    mine_pores = jnp.where(core == 0, local_pores[:, 0], local_pores[:, 1])
    columns = jnp.arange(owner_width, dtype=jnp.int32)

    swap = [(i, i ^ 1) for i in range(col_count)]
    along_x = [(i, i ^ 1) for i in range(row_count)]
    along_y = [(i, i ^ 2) for i in range(row_count)]
    ends = [(i, i ^ 2) for i in range(col_count)]
    inward = [(2 * g + c, 2 * t + c) for g, t in ((0, 1), (3, 2)) for c in range(2)]
    outward = [(2 * g + c, 2 * t + c) for g, t in ((1, 0), (2, 3)) for c in range(2)]
    across = [(2 * g + c, 2 * t + c) for g, t in ((1, 2), (2, 1)) for c in range(2)]

    sizes = [own_rows * s // sum(STEPS) for s in STEPS]
    starts = [sum(sizes[:i]) for i in range(len(sizes))]
    count = len(sizes)
    state = [dict() for _ in sizes]

    def pick(k):
        part = slice(starts[k], starts[k] + sizes[k])
        pores = jnp.concatenate([other_pores[:, part].reshape(-1), mine_pores[:, part].reshape(-1)])
        onehot = (pores[:, None] == columns[None, :]).astype(jnp.bfloat16)
        state[k]["rows"] = lax.dot_general(
            onehot, shared["solved"], (((1,), (1,)), ((), ())), preferred_element_type=jnp.float32
        ).astype(jnp.bfloat16)

    def share(k):
        s = state[k]
        if square:
            s["rows_in"] = lax.ppermute(s["rows"], "row", along_x)
        else:
            s["rows"] = lax.psum(s["rows"], "row")

    def share_again(k):
        s = state[k]
        if square:
            s["rows"] += s.pop("rows_in")
            s["rows_in"] = lax.ppermute(s["rows"], "row", along_y)

    def multiply(k):
        s = state[k]
        rows = s.pop("rows")
        if square:
            rows += s.pop("rows_in")
        half = chips * sizes[k]
        sent, mine = (
            jnp.dot(picked, shared["solved"], preferred_element_type=jnp.float32).astype(jnp.bfloat16)
            for picked in (rows[:half], rows[half:])
        )
        n = sizes[k]
        come = lax.ppermute(sent, "col", swap)
        s["own"] = mine[:n] + come[:n]
        s["rest"] = mine[n:] + come[n:]

    def rides(k):
        return k + LATER < count - ALONE

    def leaving(k):
        s, n = state[k], sizes[k]
        return s.pop("rest")[2 * n :] + s["from_middle"][n:]

    def move_in(k):
        s = state[k]
        if line:
            sent = s["rest"]
            if k >= LATER and rides(k - LATER):
                out = leaving(k - LATER)
                n = out.shape[0]
                sent = jnp.concatenate([jnp.where(at_end, sent[:n], out), sent[n:]], axis=0)
            come = lax.ppermute(sent, "col", ends if k < count - ALONE else inward)
            if k < STAYS:
                s["from_end"] = come
            else:
                flying[k] = come

    def land(k):
        s = state[k]
        if k in flying:
            s["from_end"] = flying.pop(k)

    def move_across(k):
        s = state[k]
        if line:
            n = sizes[k]
            s["from_middle"] = lax.ppermute(s["rest"][: 2 * n] + s["from_end"][n:], "col", across)

    def move_out(k):
        s = state[k]
        if line and not rides(k):
            s["from_inner"] = lax.ppermute(leaving(k), "col", outward)

    def settle(k):
        s = state[k]
        n = sizes[k]
        own = s.pop("own")
        if line:
            here = s["from_end"][:n].astype(jnp.float32) + s["from_middle"][:n].astype(jnp.float32)
            there = state[k + LATER]["from_end"][:n] if rides(k) else s["from_inner"]
            update = own.astype(jnp.float32) + jnp.where(at_end, there.astype(jnp.float32), here)
        else:
            groups = [[2 * g + c for g in range(chips)] for c in range(2)]
            pair = jnp.concatenate([own, s["rest"]], axis=0)
            update = lax.psum_scatter(
                pair, "col", scatter_dimension=0, axis_index_groups=groups, tiled=True
            ).astype(jnp.float32)
        rows = lax.slice_in_dim(shared["out"], starts[k], starts[k] + n, axis=0)
        shared["out"] = lax.dynamic_update_slice(shared["out"], rows - update, (starts[k], 0))

    plan = {}

    def at(turn, stage, *args):
        plan.setdefault(turn, []).append((stage, args))

    for k in reversed(range(count)):
        at(k, pick, k)
        at(k + 1, share, k)
        at(k + 2, share_again, k)
        at(k + 6, land, k)
    for k in reversed(range(count)):
        at(k + 3, multiply, k)
        at(k + 6, move_across, k)
        at(k + 4, move_in, k)
        if not rides(k):
            at(k + 7, move_out, k)
        at(k + (9 if rides(k) else 8), settle, k)
    shared = {"solved": solved, "out": separator_rows}
    flying = {}
    for turn in range(max(plan) + 1):
        shared, state = lax.optimization_barrier((shared, state))
        for stage, args in plan.get(turn, ()):
            stage(*args)
    return shared["out"]


def solution(mesh):
    in_specs = (
        P(("row", "col"), None),
        P(("row", "col")),
        P(("row", "col")),
        P(("row", "col")),
        P("col", "row"),
        P(),
        P("col", None),
        P("col", "row"),
    )
    out_specs = P("col", "row")
    return jax.shard_map(
        per_device, mesh=mesh, in_specs=in_specs, out_specs=out_specs, check_vma=False
    )
```

```python
import jax
import jax.numpy as jnp
from jax import lax
from jax.sharding import PartitionSpec as P

STEPS = (3, 3, 4, 4, 4, 4, 4, 3, 2, 1)
LATER = 3
STAYS = 1
ALONE = 1


def route_throats(owners, interior, offset, conductance, row_count, owner_width):
    throats = interior.shape[0]
    slot_limit = throats // 4
    order = jnp.arange(throats, dtype=jnp.int32)
    earlier = (owners[None, :] == owners[:, None]) & (order[None, :] < order[:, None])
    rank = jnp.sum(earlier.astype(jnp.int32), axis=1)
    slot = owners * slot_limit + rank
    code = (interior * owner_width + offset + 1).astype(jnp.float32)
    slots = jnp.arange(row_count * slot_limit, dtype=jnp.int32)
    placed = slots[:, None] == slot[None, :]
    codes = jnp.sum(jnp.where(placed, code[None, :], 0.0), axis=1)
    values = jnp.sum(jnp.where(placed, conductance[None, :], 0.0), axis=1)
    block = jnp.stack(
        [codes.reshape(row_count, slot_limit), values.reshape(row_count, slot_limit)], axis=1
    )
    back = lax.all_to_all(block, "row", split_axis=0, concat_axis=0, tiled=True)
    codes = back[:, 0, :].reshape(-1).astype(jnp.int32) - 1
    values = back[:, 1, :].reshape(-1)
    return codes // owner_width, codes % owner_width, values


def add_throats(child_update, pivots, pores, values):
    values = values.astype(jnp.bfloat16)
    rows = jnp.arange(child_update.shape[0], dtype=jnp.int32)
    columns = jnp.arange(child_update.shape[1], dtype=jnp.int32)
    left = jnp.where(rows[:, None] == pivots[None, :], values[None, :], jnp.bfloat16(0))
    right = (pores[:, None] == columns[None, :]).astype(jnp.bfloat16)
    summed = jnp.dot(left, right, preferred_element_type=jnp.float32)
    return (child_update.astype(jnp.float32) + summed).astype(jnp.bfloat16)


def per_device(
    throat_owner,
    throat_interior,
    throat_offset,
    throat_conductance,
    child_update,
    panel_pores,
    interior_inverse,
    separator_rows,
):
    row_count = lax.axis_size("row")
    col_count = lax.axis_size("col")
    row_index = lax.axis_index("row")
    col_index = lax.axis_index("col")
    own_rows, owner_width = separator_rows.shape
    chips = col_count // 2
    core = col_index % 2
    chip = col_index // 2
    square = row_count == 4
    line = chips == 4
    at_end = (chip == 0) | (chip == chips - 1)

    pivots, pores, values = route_throats(
        throat_owner[:, 0],
        throat_interior,
        throat_offset,
        throat_conductance,
        row_count,
        owner_width,
    )
    coupling = add_throats(child_update, pivots, pores, values)
    solved = jnp.dot(interior_inverse, coupling, preferred_element_type=jnp.float32).astype(
        jnp.bfloat16
    )

    local_pores = (panel_pores - row_index * owner_width).reshape(chips, 2, own_rows)
    if line:
        order = jnp.array([[0, 1, 2, 3], [1, 2, 3, 0], [2, 1, 0, 3], [3, 2, 1, 0]], jnp.int32)
        local_pores = jnp.take(local_pores, order[chip], axis=0)
    other_pores = jnp.where(core == 0, local_pores[:, 1], local_pores[:, 0])
    mine_pores = jnp.where(core == 0, local_pores[:, 0], local_pores[:, 1])
    columns = jnp.arange(owner_width, dtype=jnp.int32)

    swap = [(i, i ^ 1) for i in range(col_count)]
    along_x = [(i, i ^ 1) for i in range(row_count)]
    along_y = [(i, i ^ 2) for i in range(row_count)]
    ends = [(i, i ^ 2) for i in range(col_count)]
    inward = [(2 * g + c, 2 * t + c) for g, t in ((0, 1), (3, 2)) for c in range(2)]
    outward = [(2 * g + c, 2 * t + c) for g, t in ((1, 0), (2, 3)) for c in range(2)]
    across = [(2 * g + c, 2 * t + c) for g, t in ((1, 2), (2, 1)) for c in range(2)]

    sizes = [own_rows * s // sum(STEPS) for s in STEPS]
    starts = [sum(sizes[:i]) for i in range(len(sizes))]
    count = len(sizes)
    state = [dict() for _ in sizes]

    def pick(k):
        part = slice(starts[k], starts[k] + sizes[k])
        pores = jnp.concatenate([other_pores[:, part].reshape(-1), mine_pores[:, part].reshape(-1)])
        onehot = (pores[:, None] == columns[None, :]).astype(jnp.bfloat16)
        state[k]["rows"] = lax.dot_general(
            onehot, shared["solved"], (((1,), (1,)), ((), ())), preferred_element_type=jnp.float32
        ).astype(jnp.bfloat16)

    def share(k):
        s = state[k]
        if square:
            s["rows_in"] = lax.ppermute(s["rows"], "row", along_x)
        else:
            s["rows"] = lax.psum(s["rows"], "row")

    def share_again(k):
        s = state[k]
        if square:
            s["rows"] += s.pop("rows_in")
            s["rows_in"] = lax.ppermute(s["rows"], "row", along_y)

    def multiply(k):
        s = state[k]
        rows = s.pop("rows")
        if square:
            rows += s.pop("rows_in")
        half = chips * sizes[k]
        sent, mine = (
            jnp.dot(picked, shared["solved"], preferred_element_type=jnp.float32).astype(jnp.bfloat16)
            for picked in (rows[:half], rows[half:])
        )
        n = sizes[k]
        come = lax.ppermute(sent, "col", swap)
        s["own"] = mine[:n] + come[:n]
        s["rest"] = mine[n:] + come[n:]

    def rides(k):
        return k + LATER < count - ALONE

    def leaving(k):
        s, n = state[k], sizes[k]
        return s.pop("rest")[2 * n :] + s["from_middle"][n:]

    def move_in(k):
        s = state[k]
        if line:
            sent = s["rest"]
            if k >= LATER and rides(k - LATER):
                out = leaving(k - LATER)
                n = out.shape[0]
                sent = jnp.concatenate([jnp.where(at_end, sent[:n], out), sent[n:]], axis=0)
            come = lax.ppermute(sent, "col", ends if k < count - ALONE else inward)
            if k < STAYS:
                s["from_end"] = come
            else:
                flying[k] = come

    def land(k):
        s = state[k]
        if k in flying:
            s["from_end"] = flying.pop(k)

    def move_across(k):
        s = state[k]
        if line:
            n = sizes[k]
            s["from_middle"] = lax.ppermute(s["rest"][: 2 * n] + s["from_end"][n:], "col", across)

    def move_out(k):
        s = state[k]
        if line and not rides(k):
            s["from_inner"] = lax.ppermute(leaving(k), "col", outward)

    def settle(k):
        s = state[k]
        n = sizes[k]
        own = s.pop("own")
        if line:
            here = s["from_end"][:n].astype(jnp.float32) + s["from_middle"][:n].astype(jnp.float32)
            there = state[k + LATER]["from_end"][:n] if rides(k) else s["from_inner"]
            update = own.astype(jnp.float32) + jnp.where(at_end, there.astype(jnp.float32), here)
        else:
            groups = [[2 * g + c for g in range(chips)] for c in range(2)]
            pair = jnp.concatenate([own, s["rest"]], axis=0)
            update = lax.psum_scatter(
                pair, "col", scatter_dimension=0, axis_index_groups=groups, tiled=True
            ).astype(jnp.float32)
        rows = lax.slice_in_dim(shared["out"], starts[k], starts[k] + n, axis=0)
        shared["out"] = lax.dynamic_update_slice(shared["out"], rows - update, (starts[k], 0))

    plan = {}

    def at(turn, stage, *args):
        plan.setdefault(turn, []).append((stage, args))

    for k in reversed(range(count)):
        at(k, pick, k)
        at(k + 1, share, k)
        at(k + 2, share_again, k)
        at(k + 6, land, k)
    for k in reversed(range(count)):
        at(k + 3, multiply, k)
        at(k + 6, move_across, k)
        at(k + 4, move_in, k)
        if not rides(k):
            at(k + 7, move_out, k)
        at(k + (9 if rides(k) else 8), settle, k)
    shared = {"solved": solved, "out": separator_rows}
    flying = {}
    for turn in range(max(plan) + 1):
        shared, state = lax.optimization_barrier((shared, state))
        for stage, args in plan.get(turn, ()):
            stage(*args)
    return shared["out"]


def solution(mesh):
    in_specs = (
        P(("row", "col"), None),
        P(("row", "col")),
        P(("row", "col")),
        P(("row", "col")),
        P("col", "row"),
        P(),
        P("col", None),
        P("col", "row"),
    )
    out_specs = P("col", "row")
    return jax.shard_map(
        per_device, mesh=mesh, in_specs=in_specs, out_specs=out_specs, check_vma=False
    )
```
